32 devices in a mesh: dp: 16 (over z, y, x), tensor: 2 (over core).
Axes of the slice: x: 2, y: 2, z: 4, core: 2. Of those that a mesh axis runs over, the one named last changes fastest.
Arguments:
- tokens: bfloat16 [16, 592, 1024], P('dp', 'tensor'), may hold values from -6 to 6
- token_mask: int32 [16, 592], P('dp'), may hold values from 0 to 1, as said below
- attn_norm_gain: bfloat16 [1024], P(('dp', 'tensor')), may hold values from 0.099609375 to 1.8984375
- attn_norm_shift: bfloat16 [1024], P(('dp', 'tensor')), may hold values from -2 to 2
- qkv_weight: bfloat16 [3, 1024, 1024], P(None, 'dp', 'tensor'), may hold values from -1 to 1
- qv_bias: bfloat16 [2, 1024], P(None, ('dp', 'tensor')), may hold values from -2 to 2
- out_weight: bfloat16 [1024, 1024], P('tensor', 'dp'), may hold values from -1.5 to 1.5
- out_bias: bfloat16 [1024], P(('dp', 'tensor')), may hold values from -2 to 2
- mlp_norm_gain: bfloat16 [1024], P(('dp', 'tensor')), may hold values from 0.099609375 to 1.8984375
- mlp_norm_shift: bfloat16 [1024], P(('dp', 'tensor')), may hold values from -2 to 2
- up_weight: bfloat16 [1024, 4096], P('dp', 'tensor'), may hold values from -0.1875 to 0.1875
- up_bias: bfloat16 [4096], P(('dp', 'tensor')), may hold values from -2 to 2
- down_weight: bfloat16 [4096, 1024], P('tensor', 'dp'), may hold values from -0.09375 to 0.09375
- down_bias: bfloat16 [1024], P(('dp', 'tensor')), may hold values from -2 to 2
- cotangent: bfloat16 [16, 592, 1024], P('dp', 'tensor'), may hold values from -6 to 6
Outputs:
- output: bfloat16 [16, 592, 1024], P('dp', 'tensor')
- input_gradient: bfloat16 [16, 592, 1024], P('dp', 'tensor')
- attn_norm_gain_grad: float32 [1024], P(('dp', 'tensor'))
- attn_norm_shift_grad: float32 [1024], P(('dp', 'tensor'))
- qkv_weight_grad: float32 [3, 1024, 1024], P(None, 'dp', 'tensor')
- qv_bias_grad: float32 [2, 1024], P(None, ('dp', 'tensor'))
- out_weight_grad: float32 [1024, 1024], P('tensor', 'dp')
- out_bias_grad: float32 [1024], P(('dp', 'tensor'))
- mlp_norm_gain_grad: float32 [1024], P(('dp', 'tensor'))
- mlp_norm_shift_grad: float32 [1024], P(('dp', 'tensor'))
- up_weight_grad: float32 [1024, 4096], P('dp', 'tensor')
- up_bias_grad: float32 [4096], P(('dp', 'tensor'))
- down_weight_grad: float32 [4096, 1024], P('tensor', 'dp')
- down_bias_grad: float32 [1024], P(('dp', 'tensor'))
- clipped_weight: bfloat16 [2, 1024, 1024], P(None, 'dp', 'tensor')
- clipped_bias: bfloat16 [1024], P(('dp', 'tensor'))
- head_peaks: float32 [16], replicated
The draws below stay inside these ranges and needn't reach their ends.
Inputs may be any that keep to these rules, and one draw needn't show every extreme that they name: `token_mask`: position 0 of every image is 1; positions 577 and later are 0.
All inputs are finite; a program needn't handle non-finite values.
Results may differ from the reference program's by a relative error of at most 0.017.
Values may be sent and summed in bfloat16 or wider, within the bound.
No kernel may reach another device: no remote copies, remote signals or barrier semaphores. Data moves between devices by JAX's collectives and lax.ppermute only.
A program may use at most 128 MiB of HBM per device.

```python
import math
import jax
import jax.numpy as jnp
from jax import lax

D = 1024
HEADS = 16
HEAD = 64
FF = 4096
LENGTH = 577
PADDED = 592
IMAGES = 16


def draw_token_mask(key, part):
    random_marks = jax.random.randint(key, (IMAGES, PADDED), 0, 8)
    position = jnp.arange(PADDED, dtype=jnp.int32)[None, :]
    inside = (random_marks > 0) & (position < LENGTH)
    return (inside | (position == 0)).astype(jnp.int32)


def draw_qkv_weight(key, part):
    base_key = jax.random.fold_in(key, 11)
    head_key = jax.random.fold_in(key, 12)
    entries = jax.random.truncated_normal(base_key, -6.0, 6.0, (3, D, D), jnp.float32)
    spread = jnp.exp(jax.random.uniform(head_key, (HEADS,), jnp.float32, 0.0, 0.5493))
    columns = jnp.repeat(spread, HEAD)
    factor = jnp.stack([columns, columns, jnp.ones_like(columns)])
    return (entries * factor[:, None, :] / math.sqrt(D)).astype(jnp.bfloat16)


def raised(values, key, source, target, parts, factor):
    def block_of(dim):
        return (jnp.arange(values.shape[dim]) // (values.shape[dim] // parts)).reshape((-1,) + (1,) * (values.ndim - 1 - dim))

    one_side = jax.random.permutation(key, parts)[block_of(target)]
    far = (block_of(target) + parts // 2) % parts
    return jnp.where((block_of(source) == one_side) | (block_of(source) == far), factor * values, values)


def block_levels(key, shape, split, smallest, top_value):
    gain = 1.0
    for axis_at, blocks in split:
        steps = jax.random.uniform(jax.random.fold_in(jax.random.fold_in(key, 6), axis_at), (blocks,), jnp.float32, smallest / len(split), top_value / len(split))
        gain = gain * jnp.repeat(jnp.exp(steps), shape[axis_at] // blocks).reshape((-1,) + (1,) * (len(shape) - 1 - axis_at))
    return gain


def scatter_about(key, shape, deviation, bound, pieces=(), held_as=jnp.bfloat16):
    loudness = block_levels(key, shape, pieces, -0.22, 0.18) if pieces else 1.0
    values = jax.random.normal(key, shape, jnp.float32) * deviation * loudness
    return jnp.minimum(jnp.maximum(values, -bound), bound).astype(held_as)


def heavy_noise(rng, dims, scale, limit, shards, heavy, kind=jnp.bfloat16):
    values = scale * jax.random.normal(rng, dims, jnp.float32)
    if shards:
        values = values * block_levels(rng, dims, shards, -0.22, 0.18)
    return jnp.clip(raised(values, jax.random.fold_in(rng, 3), *heavy), -limit, limit).astype(kind)


def setup_inputs(seed: int = 0) -> dict:
    key_of = jax.random.split(jax.random.key(seed), 16)
    return {
        "tokens": scatter_about(key_of[0], (IMAGES, PADDED, D), 1.0, 6.0, ((0, 16), (1, 2))),
        "token_mask": draw_token_mask(jax.random.fold_in(key_of[15], 71), 0),
        "attn_norm_gain": jnp.clip(1.0 + 0.18 * jax.random.normal(key_of[2], (D,), jnp.float32), 0.099609375, 1.8984375).astype(jnp.bfloat16),
        "attn_norm_shift": scatter_about(key_of[3], (D,), 0.3, 2.0, ((0, 32),)),
        "qkv_weight": draw_qkv_weight(jax.random.fold_in(key_of[15], 71), 0),
        "qv_bias": scatter_about(key_of[5], (2, D), 0.3, 2.0, ((1, 32),)),
        "out_weight": scatter_about(key_of[6], (D, D), (D // 64) ** -0.5, 1.5, ((0, 2), (1, 16))),
        "out_bias": scatter_about(key_of[7], (D,), 0.3, 2.0, ((0, 32),)),
        "mlp_norm_gain": jnp.clip(1.0 + 0.18 * jax.random.normal(key_of[8], (D,), jnp.float32), 0.099609375, 1.8984375).astype(jnp.bfloat16),
        "mlp_norm_shift": scatter_about(key_of[9], (D,), 0.3, 2.0, ((0, 32),)),
        "up_weight": scatter_about(key_of[10], (D, FF), D ** -0.5, 0.1875, ((0, 16), (1, 2))),
        "up_bias": scatter_about(key_of[11], (FF,), 0.3, 2.0, ((0, 32),)),
        "down_weight": scatter_about(key_of[12], (FF, D), FF ** -0.5, 0.09375, ((0, 2), (1, 16))),
        "down_bias": scatter_about(key_of[13], (D,), 0.3, 2.0, ((0, 32),)),
        "cotangent": heavy_noise(key_of[14], (IMAGES, PADDED, D), 1.0, 6.0, ((0, 16), (1, 2)), (0, 2, 16, 2.0)),
    }


@jax.custom_vjp
def low(v):
    return lax.optimization_barrier(v.astype(jnp.bfloat16)).astype(jnp.float32)

@jax.custom_vjp
def low_back(v):
    return v

def low_keep(v):
    return (low(v), None)

def low_pass(kept, grad):
    return (grad,)

def back_keep(v):
    return (v, None)

def back_low(kept, grad):
    return (low(grad),)
low.defvjp(low_keep, low_pass)
low_back.defvjp(back_keep, back_low)
eps_norm = 1e-06
clip_limit = 10.0
floor_score = -1e+30
precise = lax.Precision.HIGHEST

def product(left_side, right_side):
    return jnp.dot(left_side, right_side, precision=precise, preferred_element_type=jnp.float32)

def normalize(input_tokens, norm_gain, norm_shift):
    center = input_tokens - lax.optimization_barrier(jnp.mean(input_tokens, axis=-1, keepdims=True))
    inverse = lax.rsqrt(lax.optimization_barrier(jnp.mean(center * center, axis=-1, keepdims=True)) + eps_norm)
    return center * inverse * norm_gain + norm_shift

def forward(input_tokens, valid_rows, params):
    attn_gain, attn_shift, qkv_weight, qv_bias, out_weight, out_bias, mlp_gain, mlp_shift, up_weight, up_bias, down_weight, down_bias = params
    first_norm = low(normalize(input_tokens, attn_gain, attn_shift))
    queries = low(low_back(product(first_norm, qkv_weight[0]) + qv_bias[0]))
    key_rows = low(low_back(product(first_norm, qkv_weight[1])))
    value_rows = low(low_back(product(first_norm, qkv_weight[2]) + qv_bias[1]))
    shaped = (PADDED, HEADS, HEAD)
    raw_scores = jnp.einsum('qhd,khd->hqk', queries.reshape(shaped), key_rows.reshape(shaped), precision=precise)
    scores = low_back(raw_scores * (1.0 / math.sqrt(HEAD)))
    key_keep = valid_rows[None, None, :] > 0.5
    masked = jnp.where(key_keep, scores, floor_score)
    row_peak = lax.optimization_barrier(jnp.max(masked, axis=-1, keepdims=True))
    weights = jnp.exp(masked - row_peak)
    attention = weights / lax.optimization_barrier(jnp.sum(weights, axis=-1, keepdims=True))
    mixture = jnp.einsum('hqk,khd->qhd', low(attention), value_rows.reshape(shaped), precision=precise)
    merged = low(low_back(mixture.reshape(PADDED, D)))
    attended = low_back(product(merged, out_weight))
    middle_activation = input_tokens + attended + out_bias
    second = low(normalize(middle_activation, mlp_gain, mlp_shift))
    up_pre = low_back(product(second, up_weight) + up_bias)
    active = low(jax.nn.gelu(up_pre, approximate=False))
    branch = low_back(product(active, down_weight))
    result = valid_rows[:, None] * (middle_activation + branch + down_bias)
    pair_keep = key_keep & (valid_rows[None, :, None] > 0.5)
    head_peak = lax.optimization_barrier(jnp.max(jnp.where(pair_keep, scores, floor_score), axis=(1, 2)))
    return (result, head_peak)

def reference(tokens, token_mask, attn_norm_gain, attn_norm_shift, qkv_weight, qv_bias, out_weight, out_bias, mlp_norm_gain, mlp_norm_shift, up_weight, up_bias, down_weight, down_bias, cotangent):
    params = (attn_norm_gain.astype(jnp.float32), attn_norm_shift.astype(jnp.float32), qkv_weight.astype(jnp.float32), qv_bias.astype(jnp.float32), out_weight.astype(jnp.float32), out_bias.astype(jnp.float32), mlp_norm_gain.astype(jnp.float32), mlp_norm_shift.astype(jnp.float32), up_weight.astype(jnp.float32), up_bias.astype(jnp.float32), down_weight.astype(jnp.float32), down_bias.astype(jnp.float32))

    def per_image(state_pair, slice_item):
        grad_sums, head_peaks = state_pair
        image_rows, image_mask, image_cot = slice_item
        valid_rows = image_mask.astype(jnp.float32)

        def local_block(input_tokens, weights_all):
            return forward(input_tokens, valid_rows, weights_all)
        result, pullback, head_peak = jax.vjp(local_block, image_rows.astype(jnp.float32), params, has_aux=True)
        grad_rows, grad_params = pullback(image_cot.astype(jnp.float32))
        grad_sums = jax.tree.map(lambda running, addend: running + addend, grad_sums, grad_params)
        return ((grad_sums, jnp.maximum(head_peaks, head_peak)), (result.astype(jnp.bfloat16), grad_rows.astype(jnp.bfloat16)))
    zero_sums = jax.tree.map(jnp.zeros_like, params)
    start_state = (zero_sums, jnp.full((HEADS,), floor_score, jnp.float32))
    final_state, stacked = lax.scan(per_image, start_state, (tokens, token_mask, cotangent))
    grad_sums, head_peaks = final_state
    output, input_gradient = stacked
    root_factor = jnp.sqrt(clip_limit / jnp.maximum(head_peaks, clip_limit))
    columns = jnp.repeat(root_factor, HEAD)
    clipped_weight = (qkv_weight[0:2].astype(jnp.float32) * columns).astype(jnp.bfloat16)
    clipped_bias = (qv_bias[0].astype(jnp.float32) * columns).astype(jnp.bfloat16)
    return (output, input_gradient, grad_sums[0], grad_sums[1], grad_sums[2], grad_sums[3], grad_sums[4], grad_sums[5], grad_sums[6], grad_sums[7], grad_sums[8], grad_sums[9], grad_sums[10], grad_sums[11], clipped_weight, clipped_bias, head_peaks)
```

```python
import math

import jax
import jax.numpy as jnp
from jax import lax
from jax.sharding import PartitionSpec as P

HEADS = 16
HEAD = 64


eps_norm = 1e-06
clip_limit = 10.0
floor_score = -1e30
inv_root_two = 0.7071067811865476
inv_root_two_pi = 0.3989422804014327
PARTS = 2
f32 = jnp.float32
bf16 = jnp.bfloat16


def dot(a, b, ca, cb):
    return lax.dot_general(a, b, (((ca,), (cb,)), ((), ())), preferred_element_type=f32)


def norm_statistics(rows):
    center = rows - jnp.mean(rows, axis=-1, keepdims=True)
    inverse = lax.rsqrt(jnp.mean(center * center, axis=-1, keepdims=True) + eps_norm)
    return center * inverse, inverse


def norm_pullback(grad_rows, normed, inverse, norm_gain):
    scaled = grad_rows * norm_gain
    return inverse * (
        scaled
        - jnp.mean(scaled, axis=-1, keepdims=True)
        - normed * jnp.mean(scaled * normed, axis=-1, keepdims=True)
    )


class Cube:
    def __init__(self):
        self.size = lax.axis_size("dp")
        self.count = self.size.bit_length() - 1
        index = lax.axis_index("dp")
        self.bits = [(index >> b) & 1 for b in range(self.count)]
        high = list(range(self.count - 1, 1, -1))
        self.orders = (high + [0, 1], high + [1, 0])

    def swap(self, value, bit):
        pairs = [(i, i ^ (1 << bit)) for i in range(self.size)]
        return lax.ppermute(value, "dp", pairs)

    def gather(self, shard, order):
        held = []
        value = shard
        tail = shard.shape
        for bit in order:
            other = self.swap(value, bit)
            place = sum(1 for h in held if h > bit)
            mine = self.bits[bit]
            low = jnp.where(mine == 0, value, other)
            high = jnp.where(mine == 0, other, value)
            value = jnp.stack([low, high], axis=place)
            held.append(bit)
        return value.reshape((self.size * tail[0],) + tail[1:])

    def scatter(self, value, order, wire):
        rows = value.shape[0] // self.size
        tail = value.shape[1:]
        value = value.reshape((2,) * self.count + (rows,) + tail)
        held = sorted(range(self.count), reverse=True)
        for bit in order:
            place = held.index(bit)
            mine = self.bits[bit]
            send = lax.dynamic_index_in_dim(value, 1 - mine, place, keepdims=False)
            keep = lax.dynamic_index_in_dim(value, mine, place, keepdims=False)
            value = keep.astype(f32) + self.swap(send.astype(wire), bit).astype(f32)
            held.remove(bit)
        return value


def swap_cores(value):
    return lax.ppermute(value, "tensor", [(0, 1), (1, 0)])


def local(
    tokens,
    token_mask,
    attn_norm_gain,
    attn_norm_shift,
    qkv_weight,
    qv_bias,
    out_weight,
    out_bias,
    mlp_norm_gain,
    mlp_norm_shift,
    up_weight,
    up_bias,
    down_weight,
    down_bias,
    cotangent,
):
    cube = Cube()
    ti = lax.axis_index("tensor")
    own_rows, width = tokens.shape[1:]
    padded = 2 * own_rows
    half = width // 2
    hidden_half = up_weight.shape[1]
    local_heads = half // HEAD
    part_heads = local_heads // PARTS
    part_cols = half // PARTS
    part_hidden = hidden_half // PARTS
    scale_score = 1.0 / math.sqrt(HEAD)
    dp_size = cube.size

    def both_rows(rows):
        other = swap_cores(rows)
        low = jnp.where(ti == 0, rows, other)
        high = jnp.where(ti == 0, other, rows)
        return jnp.concatenate([low, high], axis=0)

    def own_half(rows):
        return lax.dynamic_slice_in_dim(rows, ti * own_rows, own_rows, 0)

    def other_half(rows):
        return lax.dynamic_slice_in_dim(rows, (1 - ti) * own_rows, own_rows, 0)

    pieces = (
        attn_norm_gain,
        attn_norm_shift,
        qv_bias[0],
        qv_bias[1],
        out_bias,
        mlp_norm_gain,
        mlp_norm_shift,
        down_bias,
        up_bias,
    )
    sizes = [piece.shape[0] for piece in pieces]
    pack = jnp.concatenate(pieces)[None, :]
    pack = both_rows_vector(pack, ti)
    pack = cube.gather(pack[None], cube.orders[0])
    vectors = []
    start = 0
    for size in sizes:
        vectors.append(pack[:, :, start : start + size].reshape(-1).astype(f32))
        start += size
    gain1, shift1, bias_q, bias_v, bias_out, gain2, shift2, bias_down, bias_up = vectors
    bias_q_own = lax.dynamic_slice_in_dim(bias_q, ti * half, half, 0)
    bias_v_own = lax.dynamic_slice_in_dim(bias_v, ti * half, half, 0)
    bias_up_own = lax.dynamic_slice_in_dim(bias_up, ti * hidden_half, hidden_half, 0)

    out_t = out_weight.T
    down_t = down_weight.T
    attn_w, up_w, down_w = [], [], []
    for p in range(PARTS):
        cols = slice(p * part_cols, (p + 1) * part_cols)
        shard = jnp.concatenate(
            [qkv_weight[0][:, cols], qkv_weight[1][:, cols], qkv_weight[2][:, cols], out_t[:, cols]],
            axis=1,
        )
        attn_w.append(cube.gather(shard, cube.orders[p]))
    for p in range(PARTS):
        cols = slice(p * part_hidden, (p + 1) * part_hidden)
        up_w.append(cube.gather(up_weight[:, cols], cube.orders[p]))
    for p in range(PARTS):
        cols = slice(p * part_hidden, (p + 1) * part_hidden)
        down_w.append(cube.gather(down_t[:, cols], cube.orders[p]))

    row_mask = token_mask[0].astype(f32)
    x = both_rows(tokens[0]).astype(f32)
    e16 = (both_rows(cotangent[0]).astype(f32) * row_mask[:, None]).astype(bf16)
    own_mask = own_half(row_mask)

    normed1, inverse1 = norm_statistics(x)
    a1 = (normed1 * gain1 + shift1).astype(bf16)
    valid = row_mask > 0.5

    saved = []
    partial = 0.0
    peaks = []
    for p in range(PARTS):
        cols = slice(p * part_cols, (p + 1) * part_cols)
        product = dot(a1, attn_w[p][:, : 3 * part_cols], 1, 0)
        q, k, v = (product[:, i * part_cols : (i + 1) * part_cols] for i in range(3))
        q = (q + bias_q_own[cols]).astype(bf16).reshape(padded, part_heads, HEAD)
        k = k.astype(bf16).reshape(padded, part_heads, HEAD)
        v = (v + bias_v_own[cols]).astype(bf16).reshape(padded, part_heads, HEAD)
        scores = jnp.einsum("qhd,khd->hqk", q, k, preferred_element_type=f32) * scale_score
        masked = jnp.where(valid[None, None, :], scores, floor_score)
        row_peak = jnp.max(masked, axis=-1, keepdims=True)
        weights = jnp.exp(masked - row_peak)
        totals = jnp.sum(weights, axis=-1, keepdims=True)
        attention = (weights / totals).astype(bf16)
        o = jnp.einsum("hqk,khd->qhd", attention, v, preferred_element_type=f32)
        o = o.reshape(padded, part_cols).astype(bf16)
        log_total = row_peak + jnp.log(totals)
        peaks.append(jnp.max(jnp.where(valid[None, :], row_peak[:, :, 0], floor_score), axis=1))
        partial = partial + dot(o, attn_w[p][:, 3 * part_cols :], 1, 1)
        saved.append((q, k, v, o, log_total))

    hmid = x + (partial + swap_cores(partial.astype(bf16)).astype(f32)) + bias_out
    normed2, inverse2 = norm_statistics(hmid)
    a2 = (normed2 * gain2 + shift2).astype(bf16)

    peak_slots = jnp.full((HEADS,), floor_score, f32)
    peak_slots = lax.dynamic_update_slice(
        peak_slots, jnp.concatenate(peaks), (ti * local_heads,)
    )
    peak_slots = jnp.maximum(peak_slots, swap_cores(peak_slots))
    for bit in cube.orders[0]:
        peak_slots = jnp.maximum(peak_slots, cube.swap(peak_slots, bit))
    head_peaks = peak_slots

    branch = 0.0
    da2_partial = 0.0
    up_sums, up_grads, down_grads = [], [], []
    for p in range(PARTS):
        cols = slice(p * part_hidden, (p + 1) * part_hidden)
        u = dot(a2, up_w[p], 1, 0) + bias_up_own[cols]
        normal_cdf = 0.5 * (1.0 + lax.erf(u * inv_root_two))
        density = jnp.exp(-0.5 * u * u) * inv_root_two_pi
        g = (u * normal_cdf).astype(bf16)
        slope = normal_cdf + u * density
        down_grads.append(cube.scatter(dot(e16, g, 0, 0).astype(bf16), cube.orders[1 - p][::-1], bf16))
        du = (dot(e16, down_w[p], 1, 0) * slope).astype(bf16)
        up_sums.append(jnp.sum(du.astype(f32), axis=0))
        up_grads.append(cube.scatter(dot(a2, du, 0, 0).astype(bf16), cube.orders[1 - p][::-1], bf16))
        da2_partial = da2_partial + dot(du, up_w[p], 1, 1)
        branch = branch + dot(g, down_w[p], 1, 1)

    da2 = da2_partial + swap_cores(da2_partial.astype(bf16)).astype(f32)
    e = e16.astype(f32)
    dh = e + norm_pullback(da2, normed2, inverse2, gain2)
    dhb = dh.astype(bf16)

    da1_partial = 0.0
    qv_sums, attn_grads = [], []
    for p in range(PARTS):
        q, k, v, o, log_total = saved[p]
        do = dot(dhb, attn_w[p][:, 3 * part_cols :], 1, 0).astype(bf16)
        do = do.reshape(padded, part_heads, HEAD)
        scores = jnp.einsum("qhd,khd->hqk", q, k, preferred_element_type=f32) * scale_score
        masked = jnp.where(valid[None, None, :], scores, floor_score)
        attention = jnp.exp(masked - log_total)
        attention_grad = jnp.einsum("qhd,khd->hqk", do, v, preferred_element_type=f32)
        inner = jnp.sum(attention * attention_grad, axis=-1, keepdims=True)
        ds = (attention * (attention_grad - inner)).astype(bf16)
        dv = jnp.einsum("hqk,qhd->khd", attention.astype(bf16), do, preferred_element_type=f32)
        dq = jnp.einsum("hqk,khd->qhd", ds, k, preferred_element_type=f32) * scale_score
        dk = jnp.einsum("hqk,qhd->khd", ds, q, preferred_element_type=f32) * scale_score
        dqkv = jnp.concatenate(
            [dq.reshape(padded, part_cols), dk.reshape(padded, part_cols), dv.reshape(padded, part_cols)],
            axis=1,
        ).astype(bf16)
        grad = jnp.concatenate(
            [dot(a1, dqkv, 0, 0).astype(bf16), dot(dhb, o, 0, 0).astype(bf16)], axis=1
        )
        attn_grads.append(cube.scatter(grad, cube.orders[1 - p][::-1], bf16))
        da1_partial = da1_partial + dot(dqkv, attn_w[p][:, : 3 * part_cols], 1, 1)
        sums = jnp.sum(dqkv.astype(f32), axis=0)
        qv_sums.append((sums[:part_cols], sums[2 * part_cols :]))

    output = own_mask[:, None] * (
        own_half(hmid)
        + (own_half(branch) + swap_cores(other_half(branch).astype(bf16)).astype(f32))
        + bias_down
    )
    da1 = own_half(da1_partial) + swap_cores(other_half(da1_partial).astype(bf16)).astype(f32)
    own_normed1 = own_half(normed1)
    own_dh = own_half(dh)
    input_gradient = own_dh + norm_pullback(da1, own_normed1, own_half(inverse1), gain1)
    own_da2 = own_half(da2)

    def slots(own, length):
        return lax.dynamic_update_slice(jnp.zeros((length,), f32), own, (ti * own.shape[0],))

    sums = (
        jnp.sum(da1 * own_normed1, axis=0),
        jnp.sum(da1, axis=0),
        slots(jnp.concatenate([s[0] for s in qv_sums]), width),
        slots(jnp.concatenate([s[1] for s in qv_sums]), width),
        jnp.sum(own_dh, axis=0),
        jnp.sum(own_da2 * own_half(normed2), axis=0),
        jnp.sum(own_da2, axis=0),
        jnp.sum(own_half(e), axis=0),
        slots(jnp.concatenate(up_sums), 2 * hidden_half),
    )
    table = jnp.concatenate([s.reshape(dp_size, 2, -1) for s in sums], axis=2)
    mine = lax.dynamic_index_in_dim(table, ti, 1, keepdims=False)
    theirs = lax.dynamic_index_in_dim(table, 1 - ti, 1, keepdims=False)
    table = mine + swap_cores(theirs)
    total = cube.scatter(table, cube.orders[0][::-1], f32)[0]
    grads = []
    start = 0
    for size in sizes:
        grads.append(total[start : start + size])
        start += size
    (
        attn_gain_grad,
        attn_shift_grad,
        q_bias_grad,
        v_bias_grad,
        out_bias_grad,
        mlp_gain_grad,
        mlp_shift_grad,
        down_bias_grad,
        up_bias_grad,
    ) = grads

    qkv_weight_grad = jnp.stack(
        [
            jnp.concatenate([g[:, i * part_cols : (i + 1) * part_cols] for g in attn_grads], axis=1)
            for i in range(3)
        ]
    )
    out_weight_grad = jnp.concatenate([g[:, 3 * part_cols :] for g in attn_grads], axis=1).T
    up_weight_grad = jnp.concatenate(up_grads, axis=1)
    down_weight_grad = jnp.concatenate(down_grads, axis=1).T

    root_factor = jnp.sqrt(clip_limit / jnp.maximum(head_peaks, clip_limit))
    columns = jnp.repeat(root_factor, HEAD)
    own_columns = lax.dynamic_slice_in_dim(columns, ti * half, half, 0)
    clipped_weight = (qkv_weight[0:2].astype(f32) * own_columns[None, None, :]).astype(bf16)
    piece_length = qv_bias.shape[1]
    bias_columns = lax.dynamic_slice_in_dim(
        columns, lax.axis_index(("dp", "tensor")) * piece_length, piece_length, 0
    )
    clipped_bias = (qv_bias[0].astype(f32) * bias_columns).astype(bf16)
    return (
        output.astype(bf16)[None],
        input_gradient.astype(bf16)[None],
        attn_gain_grad,
        attn_shift_grad,
        qkv_weight_grad,
        jnp.stack([q_bias_grad, v_bias_grad]),
        out_weight_grad,
        out_bias_grad,
        mlp_gain_grad,
        mlp_shift_grad,
        up_weight_grad,
        up_bias_grad,
        down_weight_grad,
        down_bias_grad,
        clipped_weight,
        clipped_bias,
        head_peaks,
    )


def both_rows_vector(pack, ti):
    other = swap_cores(pack)
    low = jnp.where(ti == 0, pack, other)
    high = jnp.where(ti == 0, other, pack)
    return jnp.concatenate([low, high], axis=0)


def solution(mesh):
    in_specs = (
        P("dp", "tensor", None),
        P("dp", None),
        P(("dp", "tensor")),
        P(("dp", "tensor")),
        P(None, "dp", "tensor"),
        P(None, ("dp", "tensor")),
        P("tensor", "dp"),
        P(("dp", "tensor")),
        P(("dp", "tensor")),
        P(("dp", "tensor")),
        P("dp", "tensor"),
        P(("dp", "tensor")),
        P("tensor", "dp"),
        P(("dp", "tensor")),
        P("dp", "tensor", None),
    )
    out_specs = (
        P("dp", "tensor", None),
        P("dp", "tensor", None),
        P(("dp", "tensor")),
        P(("dp", "tensor")),
        P(None, "dp", "tensor"),
        P(None, ("dp", "tensor")),
        P("tensor", "dp"),
        P(("dp", "tensor")),
        P(("dp", "tensor")),
        P(("dp", "tensor")),
        P("dp", "tensor"),
        P(("dp", "tensor")),
        P("tensor", "dp"),
        P(("dp", "tensor")),
        P(None, "dp", "tensor"),
        P(("dp", "tensor")),
        P(),
    )
    return jax.shard_map(local, mesh=mesh, in_specs=in_specs, out_specs=out_specs, check_vma=False)
```
